768 devices in a mesh: wide: 48 (over z, y_hi, core), blk: 16 (over x, y_lo).
Axes of the slice: x: 4, y: 8 (y_hi: 2, y_lo: 4; y = y_hi * 4 + y_lo), z: 12, core: 2. Of those that a mesh axis runs over, the one named last changes fastest.
Arguments:
- query_emb: bfloat16 [3072, 4096], P(('wide', 'blk')), may hold values from -0.1875 to 0.1875
- passage_emb: bfloat16 [3072, 4096], P(('wide', 'blk')), may hold values from -0.1875 to 0.1875
- row_lse: float32 [3072], P('wide'), may hold values from 2.5 to 4.5
- positive: int32 [3072], P('wide'), may hold values from 0 to 63
- token_lengths: int32 [48, 64], P('wide'), may hold values from 1 to 16, 192 in all within a row
- destination: int32 [9216, 1], P('wide'), may hold values from 0 to 47; in each aligned block of 192 rows (0 to 191, 192 to 383, ...) at most 6 rows name the same one
- mlp_act: bfloat16 [9216, 12288], P('wide', 'blk'), may hold values from -6 to 6
- resid: bfloat16 [9216, 4096], P('wide', 'blk'), may hold values from -6 to 6
- w_down: bfloat16 [12288, 4096], P('blk'), may hold values from -0.054126588 to 0.054126588
- gain: float32 [4096], P('blk'), may hold values from 0.1 to 1.9
Outputs:
- query_grad: bfloat16 [3072, 4096], P(('wide', 'blk'))
- resid_grad: bfloat16 [13824, 4096], P('wide', 'blk')
- act_grad: bfloat16 [13824, 12288], P('wide', 'blk')
- normed_out: bfloat16 [13824, 4096], P('wide', 'blk')
The draws below stay inside these ranges and needn't reach their ends.
Inputs may be any that keep to these rules, and one draw needn't show every extreme that they name: `token_lengths`: each row lists the token counts of the group's 64 passages in order and sums to 192. Among the token rows of one group, at most 6 name the same destination.
All inputs are finite; a program needn't handle non-finite values.
Results may differ from the reference program's by a relative error of at most 0.02.
Values may be sent and summed in bfloat16 or wider, within the bound.
A program may use at most 32 MiB of HBM per device.

```python
import math
import jax
import jax.numpy as jnp
import numpy as np
from jax import lax

D = 4096
FF = 12288
TOK_DEV = 192
LMAX = 16
NPG = 64
HB = 256
FB = 768
SLOT = 6
RECV = 288
ROWS = 3072
TOKENS = 9216
OUTROWS = 13824
N_WIDE = 48
N_BLK = 16


def shared_direction(key):
    return jnp.clip(jax.random.normal(jax.random.fold_in(key, 7001), (D,), jnp.float32), -3.0, 3.0)


def unit_signs(key, count):
    picks = jax.random.randint(key, (count,), 0, 2)
    return (2 * picks - 1).astype(jnp.float32)


def hidden_signs(key):
    return unit_signs(jax.random.fold_in(key, 7002), FF)


def draw_w_down(key, part):
    limit = 6.0 * FF ** (-0.5)
    base_key = jax.random.fold_in(key, 7003)
    base = jax.random.normal(base_key, (FF, D), jnp.float32)
    common = 2.5 / FF * hidden_signs(key)[:, None] * shared_direction(key)[None, :]
    values = base * FF ** (-0.5) + common
    return jnp.clip(values, -limit, limit).astype(jnp.bfloat16)


def draw_mlp_act(key, part):
    noise_key = jax.random.fold_in(key, 7004)
    size_key = jax.random.fold_in(key, 7005)
    sign_key = jax.random.fold_in(key, 7006)
    noise = jax.random.normal(noise_key, (TOKENS, FF), jnp.float32)
    magnitude = jax.random.uniform(size_key, (TOKENS,), jnp.float32, 0.6, 1.4)
    token_level = magnitude * unit_signs(sign_key, TOKENS)
    values = 0.8 * noise + 0.6 * token_level[:, None] * hidden_signs(key)[None, :]
    return jnp.clip(values, -6.0, 6.0).astype(jnp.bfloat16)


def draw_query_emb(key, part):
    noise_key = jax.random.fold_in(key, 7007)
    size_key = jax.random.fold_in(key, 7008)
    sign_key = jax.random.fold_in(key, 7009)
    noise = jax.random.normal(noise_key, (ROWS, D), jnp.float32)
    magnitude = jax.random.uniform(size_key, (ROWS,), jnp.float32, 0.6, 1.4)
    row_level = magnitude * unit_signs(sign_key, ROWS)
    values = 0.8 * noise + 0.6 * row_level[:, None] * shared_direction(key)[None, :]
    return (0.03125 * jnp.clip(values, -6.0, 6.0)).astype(jnp.bfloat16)


def with_ends(entries, own_key, low, top_value):
    place = [jax.random.randint(jax.random.fold_in(own_key, axis), (), 0, length) for axis, length in enumerate(entries.shape)]
    longest = entries.shape.index(max(entries.shape))
    neighbour = place[:longest] + [(place[longest] + 1) % entries.shape[longest]] + place[longest + 1:]
    return entries.at[tuple(place)].set(low).at[tuple(neighbour)].set(top_value)


def shard_levels(stream_key, shape, pieces, smallest, high):
    def one(axis_at, blocks):
        heights = jax.random.uniform(jax.random.fold_in(jax.random.fold_in(stream_key, 6), axis_at), (blocks,), jnp.float32, smallest / len(pieces), high / len(pieces))
        return jnp.repeat(jnp.exp(heights), shape[axis_at] // blocks).reshape((-1,) + (1,) * (len(shape) - axis_at - 1))

    level = one(*pieces[0])
    for cut in pieces[1:]:
        level = level * one(*cut)
    return level


def split_up(count, total, most, skew):
    portions = [(1 << 20) // math.isqrt(rank ** skew) + 1 for rank in range(2, count + 1)]
    surplus, given = total - most - (count - 1), [1] * (count - 1)
    while surplus > 0:
        movable = [i for i in range(count - 1) if given[i] < most]
        pool, left = sum([portions[i] for i in movable]), surplus
        for i in movable:
            more = min(most - given[i], max(1, left * portions[i] // pool), surplus)
            given[i] = given[i] + more
            surplus = surplus - more
    return np.array([most] + given)


def ragged_sizes(stream_key, number_of, total, most, slope):
    if number_of == 2:
        one = jax.random.randint(stream_key, (), max(1, total - most), min(most, total - 1) + 1)
        return jnp.stack([one, total - one])
    tallies = jnp.asarray(split_up(number_of, total, most, slope), jnp.int32)
    twos = (number_of - 1) // 2
    donor, sink = tallies[1:1 + 2 * twos:2], tallies[2:2 + 2 * twos:2]
    room = jnp.minimum(donor - 1, most - sink)
    moved = jax.random.randint(jax.random.fold_in(stream_key, 1), (twos,), 0, 1 << 20) % (room + 1)
    tallies = tallies.at[1:1 + 2 * twos:2].set(donor - moved).at[2:2 + 2 * twos:2].set(sink + moved)
    return tallies[jax.random.permutation(jax.random.fold_in(stream_key, 2), number_of)]


def routed_block(own_key, own, number, rows, number_of, top, bound, slope):
    ranking = jax.random.permutation(own_key, number_of)
    packed, usual = portions_of(number_of, rows * top, bound, slope, True), portions_of(number_of, rows * top, bound, slope, False)
    places = jnp.arange(number_of)

    def named(sizes, rotation):
        used = int((sizes > 0).sum())
        fixed = max(1, used // 4)
        moved = fixed + (places - fixed + rotation * (used - fixed)) % max(1, number_of - fixed)
        return jnp.zeros((number_of,), jnp.int32).at[ranking[jnp.where(places < fixed, places, moved)]].set(jnp.asarray(sizes, jnp.int32))

    sizes = jnp.where(number % 4 == 0, named(packed, number // 4), named(usual, number - number // 4 - 1))
    mixed = jax.random.permutation(jax.random.fold_in(own, 3), number_of)
    donor, receiver = mixed[0:number_of // 2 * 2:2], mixed[1:number_of // 2 * 2:2]
    room = jnp.minimum(sizes[donor] - 1, bound - sizes[receiver]) // 2
    room = jnp.where((donor == ranking[0]) | (receiver == ranking[0]) | (sizes[receiver] == 0), 0, jnp.maximum(room, 0))
    moved = jax.random.randint(jax.random.fold_in(own, 4), (number_of // 2,), 0, 1 << 20) % (room + 1)
    sizes = sizes.at[donor].add(-moved).at[receiver].add(moved)
    members = jnp.searchsorted(jnp.cumsum(sizes), jnp.arange(rows * top), side="right").astype(jnp.int32)
    grid = members.reshape(top, rows).T
    grid = grid[jax.random.permutation(jax.random.fold_in(own, 1), rows)]
    rotation = jax.random.randint(jax.random.fold_in(own, 2), (rows, 1), 0, top)
    return jnp.take_along_axis(grid, (jnp.arange(top)[None, :] + rotation) % top, axis=1)


def portions_of(number_of, total, reach, slope, full):
    portions = [(1 << 20) // math.isqrt(rank ** slope) + 1 for rank in range(1, number_of + 1)]
    largest = reach if full else min(reach, max(-(-total // number_of), total * portions[0] // sum(portions)))
    least = 1 if total - largest >= number_of - 1 else 0
    counts, rest = [largest] + [least] * (number_of - 1), total - largest - least * (number_of - 1)
    while rest > 0:
        candidates = [i for i in range(1, number_of) if counts[i] < largest] or [i for i in range(1, number_of) if counts[i] < reach]
        mass, remaining = sum([portions[i] for i in candidates]), rest
        for i in candidates:
            extra = min(reach - counts[i], max(1, remaining * portions[i] // mass), rest)
            counts[i] = counts[i] + extra
            rest = rest - extra
    return np.array(counts)


def normal_values(stream_key, extent, spread, most, split=(), kind=jnp.bfloat16):
    entries = spread * jax.random.normal(stream_key, extent, jnp.float32)
    if split:
        entries = entries * shard_levels(stream_key, extent, split, -0.22, 0.18)
    return jnp.clip(entries, -most, most).astype(kind)


def setup_inputs(seed: int = 0) -> dict:
    streams_of = jax.random.split(jax.random.key(seed), 11)
    query_emb = draw_query_emb(jax.random.fold_in(streams_of[10], 71), 0)
    passage_emb = normal_values(streams_of[1], (ROWS, D), 0.03125, 0.1875, ((0, 768),))
    row_lse = jnp.clip(2.5 + 2.0 * jax.random.uniform(streams_of[2], (ROWS,), jnp.float32) ** shard_levels(streams_of[2], (ROWS,), ((0, 48),), -0.2, 0.2), 2.5, 4.5)
    positive = with_ends(jax.random.randint(streams_of[3], (ROWS,), 0, NPG), jax.random.fold_in(streams_of[3], 1), 0, NPG - 1).astype(jnp.int32)
    token_lengths = jax.vmap(lambda own: ragged_sizes(own, NPG, TOK_DEV, LMAX, 2))(jax.random.split(streams_of[4], N_WIDE)).reshape((N_WIDE, NPG)).astype(jnp.int32)
    destination_keys = jax.random.split(jax.random.fold_in(streams_of[5], 1), TOKENS // TOK_DEV)
    destination_turns = jax.random.permutation(jax.random.fold_in(streams_of[5], 3), TOKENS // TOK_DEV)
    destination = jax.vmap(lambda own, number: routed_block(jax.random.fold_in(streams_of[5], 2), own, number, TOK_DEV, N_WIDE, 1, SLOT, 2))(destination_keys, destination_turns).reshape((TOKENS, 1))
    mlp_act = draw_mlp_act(jax.random.fold_in(streams_of[10], 71), 0)
    resid = normal_values(streams_of[7], (TOKENS, D), 1.0, 6.0, ((0, 48), (1, 16)))
    w_down = draw_w_down(jax.random.fold_in(streams_of[10], 71), 0)
    gain = jnp.clip(1.0 + 0.18 * jax.random.normal(streams_of[9], (D,), jnp.float32), 0.1, 1.9)
    return {"query_emb": query_emb, "passage_emb": passage_emb, "row_lse": row_lse, "positive": positive, "token_lengths": token_lengths, "destination": destination, "mlp_act": mlp_act, "resid": resid, "w_down": w_down, "gain": gain}


logit_scale = 24.0
norm_eps = 1e-06

def reference(query_emb, passage_emb, row_lse, positive, token_lengths, destination, mlp_act, resid, w_down, gain):
    queries = query_emb.reshape(N_WIDE, NPG, D).astype(jnp.float32)
    passages = passage_emb.reshape(N_WIDE, NPG, D).astype(jnp.float32)
    scores = logit_scale * jnp.einsum('gid,gjd->gij', queries, passages)
    lse_rows = row_lse.reshape(N_WIDE, NPG)
    pos_rows = positive.reshape(N_WIDE, NPG)
    columns = jnp.arange(NPG, dtype=jnp.int32)
    target = (pos_rows[:, :, None] == columns[None, None, :]).astype(jnp.float32)
    coef_half = lax.optimization_barrier((jnp.exp(scores - lse_rows[:, :, None]) - target).astype(jnp.bfloat16))
    coef_wide = coef_half.astype(jnp.float32)
    query_grad = (logit_scale * jnp.einsum('gij,gjd->gid', coef_wide, passages)).astype(jnp.bfloat16).reshape(ROWS, D)
    pass_grad = logit_scale * jnp.einsum('gij,gid->gjd', coef_wide, queries)
    lengths = token_lengths.astype(jnp.int32)
    starts = jnp.cumsum(lengths, axis=1) - lengths
    positions = jnp.arange(TOK_DEV, dtype=jnp.int32)
    member = (positions[None, :, None] >= starts[:, None, :]) & (positions[None, :, None] < (starts + lengths)[:, None, :])
    weights = member.astype(jnp.float32) * (1.0 / lengths.astype(jnp.float32))[:, None, :]
    tok_grad = jnp.einsum('gtj,gjd->gtd', weights, pass_grad, precision=lax.Precision.HIGHEST).astype(jnp.bfloat16)
    targets = destination.reshape(N_WIDE, TOK_DEV).astype(jnp.int32)
    dest_hot = (targets[:, :, None] == jnp.arange(N_WIDE, dtype=jnp.int32)[None, None, :]).astype(jnp.int32)
    rank_of = jnp.cumsum(dest_hot, axis=1) - dest_hot
    slot_of = lax.optimization_barrier(jnp.sum(rank_of * dest_hot, axis=2))
    groups = jnp.arange(N_WIDE, dtype=jnp.int32)[:, None]
    out_index = (targets * RECV + groups * SLOT + slot_of).reshape(-1)
    blocks = w_down.reshape(N_BLK, FB, D).astype(jnp.float32)
    picker = jnp.eye(N_BLK, dtype=jnp.float32)

    def layer(inputs):
        act_rows, resid_rows, grad_rows = inputs
        partial_terms = jnp.einsum('tcf,cfd->tcd', act_rows.reshape(TOK_DEV, N_BLK, FB).astype(jnp.float32), blocks)
        placed = jnp.einsum('tch,ce->tceh', resid_rows.reshape(TOK_DEV, N_BLK, HB).astype(jnp.float32), picker).reshape(TOK_DEV, N_BLK, D)
        rounded = lax.optimization_barrier((partial_terms + placed).astype(jnp.bfloat16))
        hidden = lax.optimization_barrier(jnp.sum(rounded.astype(jnp.float32), axis=1))
        inv_rms = lax.rsqrt(lax.optimization_barrier(jnp.mean(hidden * hidden, axis=1, keepdims=True)) + norm_eps)
        normed = (gain.astype(jnp.float32)[None, :] * hidden * inv_rms).astype(jnp.bfloat16)
        gained = gain.astype(jnp.float32)[None, :] * grad_rows.astype(jnp.float32)
        inner_sum = lax.optimization_barrier(jnp.sum(gained * hidden, axis=1, keepdims=True))
        resid_back = (inv_rms * gained - hidden * (inv_rms * inv_rms * inv_rms) * inner_sum / D).astype(jnp.bfloat16)
        act_back = jnp.dot(resid_back, w_down.T, preferred_element_type=jnp.float32).astype(jnp.bfloat16)
        return (resid_back, act_back, normed)
    resid_back, act_back, normed = lax.map(layer, (mlp_act.reshape(N_WIDE, TOK_DEV, FF), resid.reshape(N_WIDE, TOK_DEV, D), tok_grad))
    resid_grad = jnp.zeros((OUTROWS, D), jnp.bfloat16).at[out_index].set(resid_back.reshape(-1, D))
    act_grad = jnp.zeros((OUTROWS, FF), jnp.bfloat16).at[out_index].set(act_back.reshape(-1, FF))
    normed_out = jnp.zeros((OUTROWS, D), jnp.bfloat16).at[out_index].set(normed.reshape(-1, D))
    return (query_grad, resid_grad, act_grad, normed_out)
```

```python
import functools

import jax
import jax.numpy as jnp
from jax import lax
from jax.experimental import pallas as pl
from jax.experimental.pallas import tpu as pltpu
from jax.sharding import PartitionSpec as P

logit_scale = 24.0
norm_eps = 1e-06
MESH = pl.DeviceIdType.MESH
N = 16
F32 = jnp.float32
BF16 = jnp.bfloat16
HIGH = lax.Precision.HIGHEST
ORDER = (2, 3, 1, 0)


def nt(a, b, precision=None):
    return lax.dot_general(
        a, b, (((1,), (1,)), ((), ())), precision=precision, preferred_element_type=F32
    )


def tn(a, b, precision=None):
    return lax.dot_general(
        a, b, (((0,), (0,)), ((), ())), precision=precision, preferred_element_type=F32
    )


def iota(shape, dim):
    return lax.broadcasted_iota(jnp.int32, shape, dim)


def partner(i, m):
    if m == 0:
        return i
    if m == 1:
        return i + 1 - 2 * lax.rem(i, 2)
    if m == 2:
        return lax.rem(i + 2, 4)
    return 3 - i


def kernel(
    q_ref, p_ref, lse_ref, pos_ref, len_ref, gain_ref, act_hbm, resid_hbm, w_hbm,
    qg_ref, out_ref,
    act, resid, w, emb, emb_all, part, ra, sb, rb, sy, ry, sc, sc_all, qgs, qgr, st, st_all, ag, acc,
    ld_sem, w_sem, emb_s, emb_r, sc_s, sc_r, st_s, st_r, qg_s, qg_r,
    a_s, a_r, b_s, b_r, y_s, y_r, gy_s, gx_s, gf_s, g_r,
):
    me = lax.axis_index("blk")
    x, y = lax.div(me, 4), lax.rem(me, 4)
    xs = [partner(x, m) for m in range(4)]
    ys = [partner(y, m) for m in range(4)]
    tok, width = resid.shape
    half = tok // 2
    pairs = lse_ref.shape[1]

    def remote(src, dst, send, recv, peer):
        return pltpu.make_async_remote_copy(
            src_ref=src, dst_ref=dst, send_sem=send, recv_sem=recv,
            device_id={"blk": peer}, device_id_type=MESH,
        )

    def cols(i):
        return pl.ds(pl.multiple_of(i * width, width), width)

    def rows8(i):
        return pl.ds(pl.multiple_of(i * 8, 8), 8)

    def each_peer(body):
        def step(o, carry):
            body(lax.rem(me + o, N))
            return carry

        lax.fori_loop(1, N, step, 0)

    ld_act = pltpu.make_async_copy(act_hbm, act, ld_sem.at[0])
    ld_act.start()
    ld_resid = pltpu.make_async_copy(resid_hbm, resid, ld_sem.at[1])
    ld_resid.start()

    def ld_w(b):
        return pltpu.make_async_copy(w_hbm.at[:, cols(b)], w.at[b], w_sem.at[b])

    for m in ORDER:
        for d in range(4):
            ld_w(d * 4 + ys[m]).start()

    barrier = pltpu.get_barrier_semaphore()
    each_peer(
        lambda peer: pl.semaphore_signal(
            barrier, inc=1, device_id={"blk": peer}, device_id_type=MESH
        )
    )
    emb[0:4, :] = q_ref[...].astype(F32)
    emb[4:8, :] = p_ref[...].astype(F32)
    emb_all[rows8(me), :] = emb[:, cols(me)]

    def term(b):
        ld_w(b).wait()
        part[b] = jnp.dot(act[...], w[b], preferred_element_type=F32).astype(BF16)

    ld_act.wait()
    for d in range(4):
        term(d * 4 + ys[ORDER[0]])
    pl.semaphore_wait(barrier, N - 1)

    def emb_copy(peer):
        return remote(
            emb.at[:, cols(peer)], emb_all.at[rows8(me), :], emb_s.at[peer], emb_r.at[me], peer
        )

    def emb_got(peer):
        return remote(
            emb.at[:, cols(peer)], emb_all.at[rows8(peer), :], emb_s.at[peer], emb_r.at[peer], peer
        )

    each_peer(lambda peer: emb_copy(peer).start())

    rows = (pl.ds(0, half), pl.ds(half, half))
    first = (1, 3)

    def a_copy(k, h, s):
        m = ORDER[k]
        block = xs[first[h]] if s == 0 else xs[2]
        return remote(
            part.at[block * 4 + ys[m], rows[h]], ra.at[k, h, s],
            a_s.at[k * 4 + h * 2 + s], a_r.at[k * 4 + h * 2 + s],
            xs[first[h]] * 4 + y,
        )

    def b_copy(k, h):
        return remote(
            sb.at[k, h], rb.at[k, h], b_s.at[k * 2 + h], b_r.at[k * 2 + h],
            xs[4 - first[h]] * 4 + y,
        )

    def y_copy(k):
        m = ORDER[k]
        return remote(sy.at[k], ry.at[k], y_s.at[k], y_r.at[k], x * 4 + ys[m])

    for k in range(4):
        if k > 0:
            for d in range(4):
                term(d * 4 + ys[ORDER[k]])
        for s in (1, 0):
            for h in range(2):
                a_copy(k, h, s).start()

    each_peer(lambda peer: emb_got(peer).wait_recv())
    e16 = emb_all[...].astype(BF16)
    r_of = iota((pairs, 8 * N), 0)
    c_of = iota((pairs, 8 * N), 1)
    q_at = lax.div(r_of, 4) * 8 + lax.rem(r_of, 4)
    pick_q = (c_of == q_at).astype(F32).astype(BF16)
    pick_p = (c_of == q_at + 4).astype(F32).astype(BF16)
    q_cols = jnp.dot(pick_q, e16, preferred_element_type=F32).astype(BF16)
    p_cols = jnp.dot(pick_p, e16, preferred_element_type=F32).astype(BF16)
    sc[...] = nt(q_cols, p_cols)
    sc_all[me] = sc[...]

    def sc_copy(peer):
        return remote(sc, sc_all.at[me], sc_s.at[peer], sc_r.at[me], peer)

    def sc_got(peer):
        return remote(sc, sc_all.at[peer], sc_s.at[peer], sc_r.at[peer], peer)

    each_peer(lambda peer: sc_copy(peer).start())

    for k in range(4):
        m = ORDER[k]
        for h in range(2):
            a_copy(k, h, 1).wait_recv()
            block = xs[4 - first[h]] * 4 + ys[m]
            sb[k, h] = (
                part[block, rows[h], :].astype(F32) + ra[k, h, 1].astype(F32)
            ).astype(BF16)
            b_copy(k, h).start()

    each_peer(lambda peer: sc_got(peer).wait_recv())
    total = sc_all[0]
    for i in range(1, N):
        total = total + sc_all[i]
    scores = logit_scale * total
    eye = iota((pairs, pairs), 0) == iota((pairs, pairs), 1)
    lse = jnp.sum(jnp.where(eye, lse_ref[...], 0.0), axis=1, keepdims=True)
    pos = jnp.sum(jnp.where(eye, pos_ref[...].astype(F32), 0.0), axis=1, keepdims=True)
    target = jnp.where(pos == iota((pairs, pairs), 1).astype(F32), 1.0, 0.0)
    coef = (jnp.exp(scores - lse) - target).astype(BF16)
    rr, cc = iota((8 * N, pairs), 0), iota((8 * N, pairs), 1)
    spread = jnp.where(
        (lax.rem(rr, 8) < 4) & (cc == lax.div(rr, 8) * 4 + lax.rem(rr, 8)), 1.0, 0.0
    ).astype(BF16)
    coef_rows = jnp.dot(spread, coef, preferred_element_type=F32).astype(BF16)
    qgs[...] = logit_scale * jnp.dot(coef_rows, p_cols, preferred_element_type=F32)
    qgr[:, cols(me)] = qgs[rows8(me), :]

    def qg_copy(peer):
        return remote(
            qgs.at[rows8(peer), :], qgr.at[:, cols(me)], qg_s.at[peer], qg_r.at[me], peer
        )

    def qg_got(peer):
        return remote(
            qgs.at[rows8(peer), :], qgr.at[:, cols(peer)], qg_s.at[peer], qg_r.at[peer], peer
        )

    pass_grad = logit_scale * tn(coef, q_cols)
    lens = len_ref[...].astype(F32)
    below = jnp.where(iota((pairs, pairs), 0) < iota((pairs, pairs), 1), 1.0, 0.0)
    starts = jnp.dot(
        jnp.broadcast_to(lens, (8, pairs)), below, precision=HIGH, preferred_element_type=F32
    )[0:1, :]
    at = iota((tok, pairs), 0).astype(F32)
    weights = jnp.where((at >= starts) & (at < starts + lens), 1.0 / lens, 0.0)
    tok_grad = jnp.dot(weights, pass_grad, precision=HIGH, preferred_element_type=F32)
    gained = gain_ref[...] * tok_grad.astype(BF16).astype(F32)

    own = None
    for k in range(4):
        m = ORDER[k]
        block = x * 4 + ys[m]
        sums = []
        for h in range(2):
            a_copy(k, h, 0).wait_recv()
            b_copy(k, h).wait_recv()
            sums.append(
                part[block, rows[h], :].astype(F32)
                + ra[k, h, 0].astype(F32)
                + rb[k, h].astype(F32)
            )
        if m != 0:
            for h in range(2):
                sy[k, rows[h], :] = sums[h].astype(BF16)
            y_copy(k).start()
        else:
            own = jnp.concatenate(sums, axis=0)
    each_peer(lambda peer: qg_copy(peer).start())
    ld_resid.wait()
    hidden = own + resid[...].astype(F32)
    for k in range(3):
        y_copy(k).wait_recv()
        hidden = hidden + ry[k].astype(F32)

    ones = jnp.ones((8, width), F32)
    squares = nt(ones, hidden * hidden, HIGH)
    inner = nt(ones, gained * hidden, HIGH)
    st[...] = jnp.where(iota((8, tok), 0) == 0, squares, inner)
    st_all[me] = st[...]

    def st_copy(peer):
        return remote(st, st_all.at[me], st_s.at[peer], st_r.at[me], peer)

    def st_got(peer):
        return remote(st, st_all.at[peer], st_s.at[peer], st_r.at[peer], peer)

    each_peer(lambda peer: st_copy(peer).start())
    each_peer(lambda peer: st_got(peer).wait_recv())
    stat = st_all[0]
    for i in range(1, N):
        stat = stat + st_all[i]
    features = N * width
    row = iota((8, tok), 0)
    inv = lax.rsqrt(stat / features + norm_eps)[0:1, :]
    scale = inv * inv * inv * stat[1:2, :] / features
    both = jnp.where(row == 0, inv, jnp.where(row == 1, scale, 0.0))
    pick = iota((8, width), 0)
    inv_rms = tn(both, jnp.where(pick == 0, 1.0, 0.0), HIGH)
    scale_c = tn(both, jnp.where(pick == 1, 1.0, 0.0), HIGH)
    resid_back = (inv_rms * gained - hidden * scale_c).astype(BF16)
    ag[me] = resid_back

    def gy_copy(m):
        return remote(ag.at[me], ag.at[me], gy_s.at[m], g_r.at[me * 2], x * 4 + ys[m])

    def gy_got(m):
        b = x * 4 + ys[m]
        return remote(ag.at[b], ag.at[b], gy_s.at[m], g_r.at[b * 2], b)

    def gx_copy(m, n):
        b = x * 4 + ys[m]
        return remote(
            ag.at[b], ag.at[b], gx_s.at[m * 2 + n // 2], g_r.at[b * 2], xs[n] * 4 + y
        )

    def gx_got(m, n):
        b = xs[n] * 4 + ys[m]
        return remote(
            ag.at[b], ag.at[b], gx_s.at[m * 2 + n // 2], g_r.at[b * 2], xs[n] * 4 + y
        )

    def gf_copy(m, h):
        b = xs[4 - first[h]] * 4 + ys[m]
        return remote(
            ag.at[b, rows[h]], ag.at[b, rows[h]], gf_s.at[m * 2 + h], g_r.at[b * 2 + h],
            xs[first[h]] * 4 + y,
        )

    def gf_got(m, h):
        b = xs[2] * 4 + ys[m]
        return remote(
            ag.at[b, rows[h]], ag.at[b, rows[h]], gf_s.at[m * 2 + h], g_r.at[b * 2 + h],
            xs[first[h]] * 4 + y,
        )

    for m in (2, 3, 1):
        gy_copy(m).start()
    for n in (1, 3):
        gx_copy(0, n).start()
    normed = (gain_ref[...] * hidden * inv_rms).astype(BF16)
    out_ref[:, 3 * width : 4 * width] = resid_back
    out_ref[:, 4 * width : 5 * width] = normed
    acc[...] = nt(resid_back, w[me])

    def use(b):
        acc[...] += nt(ag[b], w[b])

    def column(m):
        gy_got(m).wait_recv()
        for n in (1, 3):
            gx_copy(m, n).start()
        use(x * 4 + ys[m])

    def neighbours(m):
        for h in range(2):
            n = 4 - first[h]
            gx_got(m, n).wait_recv()
            gf_copy(m, h).start()
        for n in (1, 3):
            use(xs[n] * 4 + ys[m])

    column(1)
    neighbours(0)
    column(2)
    neighbours(1)
    column(3)
    neighbours(2)
    neighbours(3)
    for m in range(4):
        for h in range(2):
            gf_got(m, h).wait_recv()
        use(xs[2] * 4 + ys[m])
    out_ref[:, 0 : 3 * width] = acc[...].astype(BF16)

    each_peer(lambda peer: qg_got(peer).wait_recv())
    qg_ref[...] = qgr[0:4, :].astype(BF16)

    def sent(peer):
        emb_copy(peer).wait_send()
        sc_copy(peer).wait_send()
        st_copy(peer).wait_send()
        qg_copy(peer).wait_send()

    each_peer(sent)
    for k in range(4):
        for h in range(2):
            for s in range(2):
                a_copy(k, h, s).wait_send()
            b_copy(k, h).wait_send()
            gf_copy(k, h).wait_send()
        for n in (1, 3):
            gx_copy(k, n).wait_send()
        if k < 3:
            y_copy(k).wait_send()
            gy_copy(k + 1).wait_send()


def layer(query_emb, passage_emb, lse, pos, lens, gain, act, resid, w_down):
    tok, width = resid.shape
    hid = act.shape[1]
    features = w_down.shape[1]
    pairs = lse.shape[1]
    half = tok // 2
    dma = pltpu.SemaphoreType.DMA
    vmem = pl.BlockSpec(memory_space=pltpu.VMEM)
    hbm = pl.BlockSpec(memory_space=pl.ANY)
    return pl.pallas_call(
        kernel,
        out_shape=(
            jax.ShapeDtypeStruct(query_emb.shape, BF16),
            jax.ShapeDtypeStruct((tok, hid + 2 * width), BF16),
        ),
        in_specs=[vmem] * 6 + [hbm] * 3,
        out_specs=(vmem, vmem),
        scratch_shapes=[
            pltpu.VMEM((tok, hid), BF16),
            pltpu.VMEM((tok, width), BF16),
            pltpu.VMEM((N, hid, width), BF16),
            pltpu.VMEM((8, features), F32),
            pltpu.VMEM((8 * N, width), F32),
            pltpu.VMEM((N, tok, width), BF16),
            pltpu.VMEM((4, 2, 2, half, width), BF16),
            pltpu.VMEM((4, 2, half, width), BF16),
            pltpu.VMEM((4, 2, half, width), BF16),
            pltpu.VMEM((3, tok, width), BF16),
            pltpu.VMEM((3, tok, width), BF16),
            pltpu.VMEM((pairs, pairs), F32),
            pltpu.VMEM((N, pairs, pairs), F32),
            pltpu.VMEM((8 * N, width), F32),
            pltpu.VMEM((8, features), F32),
            pltpu.VMEM((8, tok), F32),
            pltpu.VMEM((N, 8, tok), F32),
            pltpu.VMEM((N, tok, width), BF16),
            pltpu.VMEM((tok, hid), F32),
            dma((2,)), dma((N,)),
            dma((N,)), dma((N,)), dma((N,)), dma((N,)), dma((N,)), dma((N,)), dma((N,)), dma((N,)),
            dma((16,)), dma((16,)), dma((8,)), dma((8,)), dma((4,)), dma((4,)),
            dma((4,)), dma((8,)), dma((8,)), dma((2 * N,)),
        ],
        compiler_params=pltpu.CompilerParams(
            collective_id=0, has_side_effects=True, vmem_limit_bytes=48 * 1024 * 1024
        ),
    )(query_emb, passage_emb, lse, pos, lens, gain, act, resid, w_down)


def shards(
    query_emb,
    passage_emb,
    row_lse,
    positive,
    token_lengths,
    destination,
    mlp_act,
    resid,
    w_down,
    gain,
):
    tok, feat = resid.shape
    hid = mlp_act.shape[1]
    query_grad, payload = layer(
        query_emb, passage_emb, row_lse[None, :], positive[None, :], token_lengths, gain[None, :],
        mlp_act, resid, w_down,
    )
    wide_count = lax.axis_size("wide")
    slot_count = 3 * tok // (2 * wide_count)
    dest_hot = (destination == lax.broadcasted_iota(jnp.int32, (tok, wide_count), 1)).astype(F32)
    lower = (iota((tok, tok), 1) < iota((tok, tok), 0)).astype(F32)
    rank_of = jnp.dot(lower, dest_hot, preferred_element_type=F32)
    rank = jnp.sum(rank_of * dest_hot, axis=1).astype(jnp.int32)
    slot_of = rank + destination[:, 0] * slot_count
    placer = (iota((wide_count * slot_count, tok), 0) == slot_of[None, :]).astype(BF16)
    packed = jnp.dot(placer, payload, preferred_element_type=F32).astype(BF16)
    packed = packed.reshape(wide_count, slot_count, hid + 2 * feat)
    arrived = lax.all_to_all(packed, "wide", split_axis=0, concat_axis=0, tiled=True)
    arrived = arrived.reshape(wide_count * slot_count, hid + 2 * feat)
    return (
        query_grad,
        arrived[:, hid : hid + feat],
        arrived[:, :hid],
        arrived[:, hid + feat :],
    )


def solution(mesh):
    return jax.shard_map(
        shards,
        mesh=mesh,
        in_specs=(
            P(("wide", "blk"), None),
            P(("wide", "blk"), None),
            P("wide"),
            P("wide"),
            P("wide", None),
            P("wide", None),
            P("wide", "blk"),
            P("wide", "blk"),
            P("blk", None),
            P("blk"),
        ),
        out_specs=(P(("wide", "blk"), None), P("wide", "blk"), P("wide", "blk"), P("wide", "blk")),
        check_vma=False,
    )
```
